32 devices in a mesh: grp: 2 (over y), pol: 16 (over z, x, core).
Axes of the slice: x: 2, y: 2, z: 4, core: 2. Of those that a mesh axis runs over, the one named last changes fastest.
Arguments:
- shocks: float32 [6, 128, 1024], P('grp'), parts along dimension 0, may hold values from -6 to 6
- loadings: float32 [1024, 128], P('pol'), may hold values from -0.5 to 0.5
- sec_drift: float32 [1024], P('pol'), may hold values from -0.02 to 0.08
- holdings: float32 [1024, 128], P('pol'), may hold values from -0.1875 to 0.1875
- fund_of: int32 [8192, 1], P('pol'), may hold values from 0 to 127
- product_type: int32 [8192], P('pol'), may hold values from 0 to 7
- term_years: int32 [8192], P('pol'), may hold values from 1 to 3
- asset_start: float32 [8192], P('pol'), may hold values from 0.35 to 3
- liab_start: float32 [8192], P('pol'), may hold values from 0.3 to 3
- base_lapse: float32 [8], replicated, may hold values from 0.02 to 0.2
- guarantee: float32 [8], replicated, may hold values from 0 to 0.08
- lapse_draw: bfloat16 [8192, 6, 1024], P('pol', 'grp'), parts along dimension 1, may hold values from 0 to 1
Outputs:
- assets: float32 [8192, 2048], P('pol', 'grp'), parts along dimension 1
- liability: float32 [8192, 2048], P('pol', 'grp'), parts along dimension 1
- credit_rates: float32 [6, 128, 1024], P('grp', None, 'pol'), parts along dimension 0
The draws below stay inside these ranges and needn't reach their ends.
There are 2 independent parts, one for each index of `grp`. The reference program is written for one: setup_inputs(seed, part) draws one part's arguments, and reference() takes and returns one part's arrays. A program takes and returns all parts, laid end to end along the dimension named above; an argument that names none is the same for every part. Nothing has to cross between parts.
Inputs may be any that keep to these rules, and one draw needn't show every extreme that they name: `fund_of`: every fund backs at least one policy.
All inputs are finite; a program needn't handle non-finite values.
Results may differ from the reference program's by a relative error of at most 0.0003.
Values sent between devices are 32-bit elements; how exact they have to be, the bound alone decides.
A program may use at most 64 MiB of HBM per device.

```python
import math
import jax
import jax.numpy as jnp
from jax import lax

F = 128
K = 128
P_SIZE = 1024
Y = 3
NT = 8
SECURITIES = 1024
POLICIES = 8192


def draw_term_years(key, part):
    picked = jax.random.randint(key, (POLICIES,), 0, 20, dtype=jnp.int32)
    years = jnp.where(picked < Y - 1, picked + 1, Y).astype(jnp.int32)
    position = jnp.arange(POLICIES, dtype=jnp.int32)
    years = jnp.where(position < Y - 1, position + 1, years)
    return years.astype(jnp.int32)


def with_ends(drawn, key, least, top_value):
    longest = drawn.shape.index(max(drawn.shape))
    spots = []
    for shift in (0, 1):
        where = [jax.random.randint(jax.random.fold_in(key, axis), (), 0, length) for axis, length in enumerate(drawn.shape)]
        where[longest] = (where[longest] + shift) % drawn.shape[longest]
        spots.append(tuple(where))
    return drawn.at[spots[0]].set(least).at[spots[1]].set(top_value)


def steps_of(rng, extent, cuts, smallest, high):
    def one(axis_at, parts):
        heights = jax.random.uniform(jax.random.fold_in(jax.random.fold_in(rng, 6), axis_at), (parts,), jnp.float32, smallest / len(cuts), high / len(cuts))
        return jnp.repeat(jnp.exp(heights), extent[axis_at] // parts).reshape((-1,) + (1,) * (len(extent) - axis_at - 1))

    level = one(*cuts[0])
    for cut in cuts[1:]:
        level = level * one(*cut)
    return level


def choose_distinct(key, rows, count, top, lift):
    sequence = jax.random.permutation(jax.random.fold_in(key, 1), count)
    favour = sequence
    for power in range(3):
        favour = favour * favour // count
    favour = favour * lift // count
    lots = jax.random.randint(jax.random.fold_in(key, 2), (rows, count), 0, 4096) + favour
    sure = jax.random.permutation(jax.random.fold_in(key, 3), rows)[jnp.arange(count) % rows]
    lots = jnp.where(jnp.arange(rows)[:, None] == sure[None, :], 1 << 14, lots)
    priority = lots * count + jnp.arange(count)
    return lax.top_k(priority.astype(jnp.int32), top)[1].astype(jnp.int32)


def noise(stream_key, dims, deviation, reach, cuts=(), kind=jnp.bfloat16):
    entries = deviation * jax.random.normal(stream_key, dims, jnp.float32)
    if cuts:
        entries = entries * steps_of(stream_key, dims, cuts, -0.22, 0.18)
    return jnp.clip(entries, -reach, reach).astype(kind)


def setup_inputs(seed: int = 0, part: int = 0) -> dict:
    splits = jax.random.split(jax.random.key(seed), 13)
    own_keys = jax.random.split(jax.random.fold_in(splits[12], part), 13)
    return {
        "shocks": noise(own_keys[0], (Y, K, P_SIZE), 1.0, 6.0, (), jnp.float32),
        "loadings": noise(splits[1], (SECURITIES, K), K ** -0.5, 0.5, ((0, 16),), jnp.float32),
        "sec_drift": jnp.clip(-0.02 + 0.09999999776482582 * jax.random.uniform(splits[2], (SECURITIES,), jnp.float32) ** steps_of(splits[2], (SECURITIES,), ((0, 16),), -0.2, 0.2), -0.02, 0.08),
        "holdings": noise(splits[3], (SECURITIES, F), SECURITIES ** -0.5, 0.1875, ((0, 16),), jnp.float32),
        "fund_of": choose_distinct(splits[4], POLICIES, F, 1, 0),
        "product_type": with_ends(jax.random.randint(splits[5], (POLICIES,), 0, NT), jax.random.fold_in(splits[5], 1), 0, NT - 1).astype(jnp.int32),
        "term_years": draw_term_years(jax.random.fold_in(splits[12], 71), part),
        "asset_start": jnp.clip(jnp.exp(math.log(3.0) - 2.1484344 * jax.random.uniform(splits[7], (POLICIES,), jnp.float32) ** steps_of(splits[7], (POLICIES,), ((0, 16),), -0.2, 0.2)), 0.35, 3.0),
        "liab_start": jnp.clip(jnp.exp(math.log(3.0) - 2.3025851 * jax.random.uniform(splits[8], (POLICIES,), jnp.float32) ** steps_of(splits[8], (POLICIES,), ((0, 16),), -0.2, 0.2)), 0.3, 3.0),
        "base_lapse": jnp.clip(jnp.exp(jax.random.uniform(splits[9], (NT,), jnp.float32, math.log(0.02), math.log(0.2))), 0.02, 0.2),
        "guarantee": jnp.clip(jax.random.uniform(splits[10], (NT,), jnp.float32, 0.0, 0.08), 0.0, 0.08),
        "lapse_draw": jnp.clip(1.0 * jax.random.uniform(own_keys[11], (POLICIES, Y, P_SIZE), jnp.float32) ** steps_of(own_keys[11], (POLICIES, Y, P_SIZE), ((0, 16),), -0.2, 0.2), 0.0, 1.0).astype(jnp.bfloat16),
    }


def reference(shocks, loadings, sec_drift, holdings, fund_of, product_type, term_years, asset_start, liab_start, base_lapse, guarantee, lapse_draw):
    highest = lax.Precision.HIGHEST
    sec_ret = 0.25 * jnp.tanh(jnp.einsum('sk,ykp->ysp', loadings, shocks, precision=highest)) + sec_drift[None, :, None]
    fund_ret = jnp.einsum('sf,ysp->yfp', holdings, sec_ret, precision=highest)
    fund_index = fund_of[:, 0]
    guaranteed = guarantee[product_type]
    base_rate = base_lapse[product_type]
    count = asset_start.shape[0]
    assets = jnp.broadcast_to(asset_start[:, None], (count, P_SIZE))
    liability = jnp.broadcast_to(liab_start[:, None], (count, P_SIZE))
    collected = []
    for year in range(Y):
        in_force = (term_years > year).astype(jnp.float32)[:, None]
        growth = fund_ret[year][fund_index]
        assets = assets * (1.0 + in_force * growth)
        asset_sums = jax.ops.segment_sum(in_force * assets, fund_index, num_segments=F)
        liab_sums = jax.ops.segment_sum(liability, fund_index, num_segments=F)
        declared = 0.01 + jax.nn.softplus(20.0 * (asset_sums / liab_sums - 1.05)) / 20.0
        credit = jnp.maximum(declared[fund_index], guaranteed[:, None])
        lapse_rate = jnp.minimum(base_rate[:, None] * (0.5 + lapse_draw[:, year, :].astype(jnp.float32)) * jnp.exp(5.0 * (growth - credit)), 0.5)
        liability = liability * (1.0 + in_force * credit) * (1.0 - in_force * lapse_rate)
        assets = assets * (1.0 - in_force * lapse_rate)
        collected.append(declared)
    return assets, liability, jnp.stack(collected)
```

```python
import functools

import jax
import jax.numpy as jnp
from jax import lax
from jax.experimental import pallas as pl
from jax.experimental.pallas import tpu as pltpu
from jax.sharding import PartitionSpec as P

MESH = pl.DeviceIdType.MESH
HIGHEST = lax.Precision.HIGHEST


def crediting(ra, rl):
    x = 20.0 * (ra / rl - 1.05)
    return 0.01 + (jnp.maximum(x, 0.0) + jnp.log1p(jnp.exp(-jnp.abs(x)))) / 20.0


def place():
    me = lax.axis_index("pol")
    chip, core = me // 2, me % 2
    return chip, core, chip * 2 + 1 - core


def greet(chips, chip, core, partner):
    barrier = pltpu.get_barrier_semaphore()
    pl.semaphore_signal(barrier, inc=1, device_id={"pol": partner}, device_id_type=MESH)
    for t in range(1, chips):
        other = lax.rem(chip + t, chips) * 2 + core
        pl.semaphore_signal(barrier, inc=1, device_id={"pol": other}, device_id_type=MESH)
    pl.semaphore_wait(barrier, chips)


def remote(src, dst, send, recv, device):
    return pltpu.make_async_remote_copy(
        src_ref=src,
        dst_ref=dst,
        send_sem=send,
        recv_sem=recv,
        device_id={"pol": device},
        device_id_type=MESH,
    )


def spread(chips, own_ref, all_ref, chip_send, chip_recv, core_send, core_recv):
    chip, core, partner = place()
    out = []
    for t in range(1, chips):
        device = lax.rem(chip + t, chips) * 2 + core
        copy = remote(own_ref, all_ref.at[chip, core], chip_send.at[t], chip_recv.at[t], device)
        copy.start()
        out.append(copy)
    first = remote(own_ref, all_ref.at[chip, core], core_send.at[0], core_recv.at[0], partner)
    first.start()
    all_ref[chip, core] = own_ref[...]
    forwards = [first]
    for t in range(1, chips):
        source = lax.rem(chip + chips - t, chips)
        slot = all_ref.at[source, core]
        out[t - 1].wait_recv()
        forward = remote(slot, slot, core_send.at[t], core_recv.at[t], partner)
        forward.start()
        forwards.append(forward)
    for copy in forwards:
        copy.wait_recv()
    for copy in out + forwards:
        copy.wait_send()


def gather_kernel(chips, own_ref, all_ref, chip_send, chip_recv, core_send, core_recv):
    greet(chips, *place())
    spread(chips, own_ref, all_ref, chip_send, chip_recv, core_send, core_recv)


def gather(own, chips):
    return pl.pallas_call(
        functools.partial(gather_kernel, chips),
        out_shape=jax.ShapeDtypeStruct((chips, 2) + own.shape, own.dtype),
        in_specs=[pl.BlockSpec(memory_space=pltpu.VMEM)],
        out_specs=pl.BlockSpec(memory_space=pltpu.VMEM),
        scratch_shapes=[pltpu.SemaphoreType.DMA((chips,))] * 4,
        compiler_params=pltpu.CompilerParams(collective_id=0, has_side_effects=True),
        name="gather",
    )(own)


def exchange_kernel(
    chips, sums, rates, theirs, mine, arrived, own, s1, r1, s2, r2, s3, r3, s4, r4
):
    chip, core, partner = place()
    greet(chips, chip, core, partner)
    order = list(range(1, chips)) + [0]
    across = {}
    for t in order:
        j = lax.rem(chip + t, chips)
        across[t] = remote(
            sums.at[:, j, 1 - core], theirs.at[j], s1.at[t], r1.at[t], partner
        )
        across[t].start()
    out = []
    for t in range(1, chips):
        j = lax.rem(chip + t, chips)
        across[t].wait_recv()
        mine[t] = sums[:, j, core] + theirs[j]
        copy = remote(mine.at[t], arrived.at[t], s2.at[t], r2.at[t], j * 2 + core)
        copy.start()
        out.append(copy)
    across[0].wait_recv()
    total = sums[:, chip, core] + theirs[chip]
    for t in range(1, chips):
        out[t - 1].wait_recv()
        total = total + arrived[t]
    own[...] = crediting(total[0], total[1])
    spread(chips, own, rates, s3, r3, s4, r4)
    for copy in list(across.values()) + out:
        copy.wait_send()


def exchange(sums, chips):
    rows, paths = sums.shape[3:]
    part = pltpu.VMEM((chips, 2, rows, paths), jnp.float32)
    return pl.pallas_call(
        functools.partial(exchange_kernel, chips),
        out_shape=jax.ShapeDtypeStruct((chips, 2, rows, paths), jnp.float32),
        in_specs=[pl.BlockSpec(memory_space=pltpu.VMEM)],
        out_specs=pl.BlockSpec(memory_space=pltpu.VMEM),
        scratch_shapes=[part, part, part, pltpu.VMEM((rows, paths), jnp.float32)]
        + [pltpu.SemaphoreType.DMA((chips,))] * 8,
        compiler_params=pltpu.CompilerParams(collective_id=1, has_side_effects=True),
        name="exchange",
    )(sums)


def split(x):
    high = x.astype(jnp.bfloat16)
    return high, (x - high.astype(jnp.float32)).astype(jnp.bfloat16)


def dot(a, b):
    return jnp.dot(a, b, preferred_element_type=jnp.float32)


def returns_kernel(secs, every, shocks, fund_ret, first, loads, holds, cols):
    chunk = pl.program_id(1)
    last = pl.num_programs(1) - 1
    group, _, funds = every.shape
    depth = group * secs

    @pl.when(pl.program_id(0) == 0)
    def _():
        high, low = split(every[:, :secs].reshape(depth, funds))
        loads[chunk] = jnp.concatenate([high, low], axis=1)
        high, low = split(every[:, secs : 2 * secs].reshape(depth, funds).T)
        holds[chunk] = jnp.concatenate([high, low], axis=0)

    extras = jnp.sum(every[:, 2 * secs :], axis=0)
    columns = jnp.concatenate([extras, jnp.zeros((funds - 8, funds), jnp.float32)], axis=0).T

    @pl.when(chunk == 0)
    def _():
        cols[...] = columns

    @pl.when(chunk > 0)
    def _():
        cols[...] += columns

    for year in range(shocks.shape[0]):
        high, low = split(shocks[year])
        exposure = dot(loads[chunk], jnp.concatenate([high, high], axis=0)) + dot(
            loads[chunk, :, :funds], low
        )
        high, low = split(0.25 * jnp.tanh(exposure))
        both = dot(holds[chunk], high)
        term = both[:funds] + both[funds:] + dot(holds[chunk, :funds], low)

        @pl.when(chunk == 0)
        def _():
            fund_ret[year] = term

        @pl.when(chunk > 0)
        def _():
            fund_ret[year] += term

        @pl.when(chunk == last)
        def _():
            fund_ret[year] += cols[:, 0:1]

    @pl.when(chunk == last)
    def _():
        first[...] = crediting(cols[:, 1:2] * (1.0 + fund_ret[0]), cols[:, 2:3])


def returns(every, shocks, secs):
    size, height, funds = every.shape
    years, factors, paths = shocks.shape
    group = min(size, 16)
    block = min(paths, 256)
    chunks = size // group
    depth = group * secs
    return pl.pallas_call(
        functools.partial(returns_kernel, secs),
        grid=(paths // block, chunks),
        out_shape=(
            jax.ShapeDtypeStruct((years, funds, paths), jnp.float32),
            jax.ShapeDtypeStruct((funds, paths), jnp.float32),
        ),
        in_specs=[
            pl.BlockSpec((group, height, funds), lambda p, c: (c, 0, 0)),
            pl.BlockSpec((years, factors, block), lambda p, c: (0, 0, p)),
        ],
        out_specs=(
            pl.BlockSpec((years, funds, block), lambda p, c: (0, 0, p)),
            pl.BlockSpec((funds, block), lambda p, c: (0, p)),
        ),
        scratch_shapes=[
            pltpu.VMEM((chunks, depth, 2 * factors), jnp.bfloat16),
            pltpu.VMEM((chunks, 2 * funds, depth), jnp.bfloat16),
            pltpu.VMEM((funds, funds), jnp.float32),
        ],
        name="returns",
    )(every, shocks)


def local(
    shocks,
    loadings,
    sec_drift,
    holdings,
    fund_of,
    product_type,
    term_years,
    asset_start,
    liab_start,
    base_lapse,
    guarantee,
    lapse_draw,
):
    num_years, num_factors, num_paths = shocks.shape
    secs, num_funds = holdings.shape
    size = lax.axis_size("pol")
    chips = size // 2
    rows = num_funds // size
    count = asset_start.shape[0]
    member = (fund_of[:, 0][:, None] == jnp.arange(num_funds, dtype=jnp.int32)[None, :]).astype(
        jnp.float32
    )
    first_force = (term_years > 0).astype(jnp.float32)
    extras = jnp.stack(
        [
            jnp.sum(holdings * sec_drift[:, None], axis=0),
            jnp.sum(member * (first_force * asset_start)[:, None], axis=0),
            jnp.sum(member * liab_start[:, None], axis=0),
        ]
    )
    extras = jnp.pad(extras, ((0, 5), (0, 0)))
    packed = jnp.concatenate([loadings, holdings, extras], axis=0)
    everyone = gather(packed, chips).reshape(size, 2 * secs + 8, num_funds)
    fund_ret, first_rates = returns(everyone, shocks, secs)

    type_hot = (
        product_type[:, None] == jnp.arange(base_lapse.shape[0], dtype=jnp.int32)[None, :]
    ).astype(jnp.float32)
    guaranteed = jnp.sum(type_hot * guarantee[None, :], axis=1)
    base_rate = jnp.sum(type_hot * base_lapse[None, :], axis=1)
    assets = jnp.broadcast_to(asset_start[:, None], (count, num_paths))
    liability = jnp.broadcast_to(liab_start[:, None], (count, num_paths))
    owned_paths = num_paths // size
    first_path = lax.axis_index("pol") * owned_paths
    collected = []
    for year in range(num_years):
        year_ret = fund_ret[year]
        in_force = (term_years > year).astype(jnp.float32)[:, None]
        growth = jnp.dot(member, year_ret, precision=HIGHEST)
        assets = assets * (1.0 + in_force * growth)
        if year == 0:
            declared = first_rates
        else:
            sums = jnp.stack(
                [
                    jnp.dot(member.T, in_force * assets, precision=HIGHEST),
                    jnp.dot(member.T, liability, precision=HIGHEST),
                ]
            )
            declared = exchange(sums.reshape(2, chips, 2, rows, num_paths), chips).reshape(
                num_funds, num_paths
            )
        own_rates = lax.dynamic_slice_in_dim(declared, first_path, owned_paths, 1)
        collected.append(own_rates)
        credit = jnp.maximum(jnp.dot(member, declared, precision=HIGHEST), guaranteed[:, None])
        lapse_rate = jnp.minimum(
            base_rate[:, None]
            * (0.5 + lapse_draw[:, year, :].astype(jnp.float32))
            * jnp.exp(5.0 * (growth - credit)),
            0.5,
        )
        liability = liability * (1.0 + in_force * credit) * (1.0 - in_force * lapse_rate)
        assets = assets * (1.0 - in_force * lapse_rate)
    return (assets, liability, jnp.stack(collected))


def solution(mesh):
    in_specs = (
        P("grp", None, None),
        P("pol", None),
        P("pol"),
        P("pol", None),
        P("pol", None),
        P("pol"),
        P("pol"),
        P("pol"),
        P("pol"),
        P(),
        P(),
        P("pol", "grp", None),
    )
    out_specs = (P("pol", "grp"), P("pol", "grp"), P("grp", None, "pol"))
    return jax.shard_map(local, mesh=mesh, in_specs=in_specs, out_specs=out_specs, check_vma=False)
```

```python
import functools

import jax
import jax.numpy as jnp
from jax import lax
from jax.experimental import pallas as pl
from jax.experimental.pallas import tpu as pltpu
from jax.sharding import PartitionSpec as P

MESH = pl.DeviceIdType.MESH
HIGHEST = lax.Precision.HIGHEST
PARTS = 2
LANES = 256
ROWS = 256


def crediting(ra, rl):
    x = 20.0 * (ra / rl - 1.05)
    return 0.01 + (jnp.maximum(x, 0.0) + jnp.log1p(jnp.exp(-jnp.abs(x)))) / 20.0


def split(x):
    high = x.astype(jnp.bfloat16)
    return high, (x - high.astype(jnp.float32)).astype(jnp.bfloat16)


def stacked(x):
    return jnp.concatenate(split(x), axis=0)


def dot(a, b):
    return jnp.dot(a, b, preferred_element_type=jnp.float32)


class Place:
    def __init__(self, depth):
        me = lax.axis_index("pol")
        self.depth = depth
        self.core = lax.rem(me, 2)
        self.x = lax.rem(me // 2, 2)
        self.z = me // 4

    def device(self, z, x, core):
        return (z * 2 + x) * 2 + core

    def ahead(self, t):
        return lax.rem(self.z + t, self.depth)

    def behind(self, t):
        return lax.rem(self.z + self.depth - t, self.depth)

    def to_core(self):
        return self.device(self.z, self.x, 1 - self.core)

    def to_x(self):
        return self.device(self.z, 1 - self.x, self.core)

    def to_z(self, t):
        return self.device(self.ahead(t), self.x, self.core)

    def greet(self):
        barrier = pltpu.get_barrier_semaphore()
        others = [self.to_core(), self.to_x()] + [self.to_z(t) for t in range(1, self.depth)]
        for other in others:
            pl.semaphore_signal(barrier, inc=1, device_id={"pol": other}, device_id_type=MESH)
        pl.semaphore_wait(barrier, len(others))


def send(src, dst, sems, at, device):
    copy = pltpu.make_async_remote_copy(
        src_ref=src,
        dst_ref=dst,
        send_sem=sems.at[0, at],
        recv_sem=sems.at[1, at],
        device_id={"pol": device},
        device_id_type=MESH,
    )
    copy.start()
    return copy


class Spread:
    def __init__(self, place, own, every, sems):
        self.p, self.own, self.every, self.sems = place, own, every, sems

    def start(self):
        p, n = self.p, self.p.depth
        slot = self.every.at[p.z, p.x, p.core]
        self.along = [send(self.own, slot, self.sems, t, p.to_z(t)) for t in range(1, n)]
        self.across = [send(self.own, slot, self.sems, n, p.to_x())]
        self.pair = [send(self.own, slot, self.sems, 2 * n, p.to_core())]
        self.every[p.z, p.x, p.core] = self.own[...]

    def relay_z(self):
        p, n = self.p, self.p.depth
        for t in range(1, n):
            self.along[t - 1].wait_recv()
            slot = self.every.at[p.behind(t), p.x, p.core]
            self.across.append(send(slot, slot, self.sems, n + t, p.to_x()))
            self.pair.append(send(slot, slot, self.sems, 2 * n + t, p.to_core()))

    def relay_x(self):
        p, n = self.p, self.p.depth
        for t in range(n):
            self.across[t].wait_recv()
            slot = self.every.at[p.behind(t), 1 - p.x, p.core]
            self.pair.append(send(slot, slot, self.sems, 3 * n + t, p.to_core()))

    def finish(self):
        for copy in self.pair:
            copy.wait_recv()
        for copy in self.along + self.across + self.pair:
            copy.wait_send()


class Totals:
    def __init__(self, place, sums, pair_in, x_out, x_in, z_out, z_in, sems):
        self.p, self.sums, self.pair_in, self.sems = place, sums, pair_in, sems
        self.x_out, self.x_in, self.z_out, self.z_in = x_out, x_in, z_out, z_in
        self.order = list(range(1, place.depth)) + [0]

    def start(self):
        p, n = self.p, self.p.depth
        self.pair = {}
        for x, base in ((1 - p.x, 0), (p.x, n)):
            for t in self.order:
                z = p.ahead(t)
                self.pair[base + t] = send(
                    self.sums.at[:, z, x, 1 - p.core],
                    self.pair_in.at[z, x],
                    self.sems,
                    base + t,
                    p.to_core(),
                )

    def add_x(self):
        p, n = self.p, self.p.depth
        self.across = {}
        for t in self.order:
            z = p.ahead(t)
            self.pair[t].wait_recv()
            self.x_out[t] = self.sums[:, z, 1 - p.x, p.core] + self.pair_in[z, 1 - p.x]
            self.across[t] = send(
                self.x_out.at[t], self.x_in.at[t], self.sems, 2 * n + t, p.to_x()
            )

    def chip_sum(self, t):
        p, n = self.p, self.p.depth
        z = p.ahead(t)
        self.pair[n + t].wait_recv()
        self.across[t].wait_recv()
        return self.sums[:, z, p.x, p.core] + self.pair_in[z, p.x] + self.x_in[t]

    def add_z(self):
        p, n = self.p, self.p.depth
        self.along = {}
        for t in range(1, n):
            self.z_out[t] = self.chip_sum(t)
            self.along[t] = send(
                self.z_out.at[t], self.z_in.at[t], self.sems, 3 * n + t, p.to_z(t)
            )

    def finish(self):
        total = self.chip_sum(0)
        for t in range(1, self.p.depth):
            self.along[t].wait_recv()
            total = total + self.z_in[t]
        return total

    def settle(self):
        for group in (self.pair, self.across, self.along):
            for copy in group.values():
                copy.wait_send()


def year_step(member, hot, force, base, floor, growth_of, credit_of, draw, assets, liability):
    growth = dot(member, growth_of)
    credit = jnp.maximum(dot(member, credit_of), floor)
    assets = assets * (1.0 + force * growth)
    lapse = force * jnp.minimum(
        base * (0.5 + draw.astype(jnp.float32)) * jnp.exp(5.0 * (growth - credit)), 0.5
    )
    stay = 1.0 - lapse
    return assets * stay, liability * (1.0 + force * credit) * stay


def main_kernel(
    base_lapse,
    guarantee,
    fund_row,
    type_row,
    term_row,
    asset_row,
    liab_row,
    drift_row,
    loadings,
    holdings,
    shocks_hbm,
    draws_hbm,
    assets,
    liability,
    fund_ret,
    rates,
    member,
    columns,
    shocks,
    draws,
    packed,
    every,
    loads,
    holds,
    hots,
    extra_columns,
    sums,
    pair_in,
    x_out,
    x_in,
    z_out,
    z_in,
    own,
    local_sems,
    gather_sems,
    total_sems,
    spread_sems,
):
    depth = every.shape[0]
    secs, funds = holdings.shape
    count = fund_row.shape[1]
    years = shocks.shape[0]
    width = assets.shape[2]
    groups, group_secs, _ = loads.shape
    place = Place(depth)

    fetch_shocks = pltpu.make_async_copy(shocks_hbm, shocks, local_sems.at[0])
    fetch_draws = pltpu.make_async_copy(
        draws_hbm.at[pl.ds(0, years - 1)], draws, local_sems.at[1]
    )
    fetch_shocks.start()
    fetch_draws.start()

    fund_id = lax.broadcasted_iota(jnp.int32, (funds, count), 0)
    hot = fund_row[...] == fund_id
    hot_rows = hot.astype(jnp.float32)
    floor = jnp.zeros((1, count), jnp.float32)
    base = jnp.zeros((1, count), jnp.float32)
    for kind in range(guarantee.shape[0]):
        same = type_row[...] == kind
        floor = jnp.where(same, guarantee[kind], floor)
        base = jnp.where(same, base_lapse[kind], base)
    in_force = [(term_row[...] > year).astype(jnp.float32) for year in range(years)]
    row = lax.broadcasted_iota(jnp.int32, (funds, count), 0)
    table = jnp.zeros((funds, count), jnp.float32)
    for at, values in enumerate([floor, base, asset_row[...], liab_row[...]] + in_force):
        table = jnp.where(row == at, values, table)
    columns[...] = table.T
    starts = jnp.concatenate(
        [in_force[0] * asset_row[...], liab_row[...], jnp.zeros((6, count), jnp.float32)], axis=0
    )
    member_f32 = hot_rows.T
    start_sums = jnp.dot(starts, member_f32, precision=HIGHEST)
    drifts = jnp.broadcast_to(drift_row[...], (8, secs))
    drift_sums = jnp.dot(drifts, holdings[...], precision=HIGHEST)
    packed[:secs] = loadings[...]
    packed[secs : 2 * secs] = holdings[...]
    packed[2 * secs : 2 * secs + 8] = drift_sums
    packed[2 * secs + 8 :] = start_sums

    place.greet()
    gather = Spread(place, packed, every, gather_sems)
    gather.start()
    narrow = member_f32.astype(jnp.bfloat16)
    member[...] = jnp.concatenate([narrow, narrow], axis=1)
    hots[0] = hot_rows.astype(jnp.bfloat16)
    for year in range(1, years):
        hots[year] = jnp.where(in_force[year] > 0.0, hot_rows, 0.0).astype(jnp.bfloat16)
    gather.relay_z()
    gather.relay_x()
    gather.finish()
    fetch_shocks.wait()
    fetch_draws.wait()

    per = group_secs // secs
    flat = every.shape[0] * 4
    extra = jnp.zeros((16, funds), jnp.float32)
    for device in range(flat):
        extra += every[device // 4, (device // 2) % 2, device % 2, 2 * secs :]
    extra_columns[...] = jnp.concatenate(
        [extra, jnp.zeros((funds - 16, funds), jnp.float32)], axis=0
    ).T

    def prepare(at, _):
        block = every[at]
        high, low = split(block[:, :, :secs].reshape(group_secs, funds))
        loads[at] = jnp.concatenate([high, low], axis=1)
        high, low = split(block[:, :, secs : 2 * secs].reshape(group_secs, funds).T)
        holds[at] = jnp.concatenate([high, low], axis=0)
        return 0

    lax.fori_loop(0, groups, prepare, 0)

    def returns(part, year):
        high, low = split(shocks[year, :, part * width : (part + 1) * width])
        twice = jnp.concatenate([high, high], axis=0)

        def step(at, total):
            exposure = dot(loads[at], twice) + dot(loads[at, :, :funds], low)
            t_high, t_low = split(0.25 * jnp.tanh(exposure))
            both = dot(holds[at], t_high)
            return total + both[:funds] + both[funds:] + dot(holds[at, :funds], t_low)

        total = lax.fori_loop(0, groups, step, jnp.zeros((funds, width), jnp.float32))
        fund_ret[year, part] = total + extra_columns[:, 0:1]

    def first_rates(part):
        declared = crediting(
            extra_columns[:, 8:9] * (1.0 + fund_ret[0, part]), extra_columns[:, 9:10]
        )
        rates[0, part] = declared.reshape(rates.shape[2:])

    def advance(part, year):
        def step(block, _):
            lanes = pl.ds(pl.multiple_of(block * LANES, LANES), LANES)
            growth_of = stacked(fund_ret[year, part, :, lanes])
            declared = rates[year, part, :, :, :, :, lanes].reshape(funds, LANES)
            credit_of = stacked(declared)
            asset_sum = jnp.zeros((funds, LANES), jnp.float32)
            liab_sum = jnp.zeros((funds, LANES), jnp.float32)
            for first in range(0, count, ROWS):
                rows = slice(first, first + ROWS)
                if year == 0:
                    held = jnp.broadcast_to(columns[rows, 2:3], (ROWS, LANES))
                    owed = jnp.broadcast_to(columns[rows, 3:4], (ROWS, LANES))
                else:
                    held = assets[part, rows, lanes]
                    owed = liability[part, rows, lanes]
                draw_at = pl.ds(pl.multiple_of(part * width + block * LANES, LANES), LANES)
                held, owed = year_step(
                    member[rows],
                    None,
                    columns[rows, 4 + year : 5 + year],
                    columns[rows, 1:2],
                    columns[rows, 0:1],
                    growth_of,
                    credit_of,
                    draws[year, rows, draw_at],
                    held,
                    owed,
                )
                assets[part, rows, lanes] = held
                liability[part, rows, lanes] = owed
                high, low = split(held)
                pick = hots[year + 1, :, rows]
                asset_sum += dot(pick, high) + dot(pick, low)
                high, low = split(owed)
                pick = hots[0, :, rows]
                liab_sum += dot(pick, high) + dot(pick, low)
            asset_sum = asset_sum * (1.0 + fund_ret[year + 1, part, :, lanes])
            shape = sums.shape[2:6] + (LANES,)
            sums[part, 0, :, :, :, :, lanes] = asset_sum.reshape(shape)
            sums[part, 1, :, :, :, :, lanes] = liab_sum.reshape(shape)
            return 0

        lax.fori_loop(0, width // LANES, step, 0)

    def totals(part):
        return Totals(
            place,
            sums.at[part],
            pair_in.at[part],
            x_out.at[part],
            x_in.at[part],
            z_out.at[part],
            z_in.at[part],
            total_sems.at[part],
        )

    def declare(total, year, part):
        summed = total.finish()
        own[part] = crediting(summed[0], summed[1])
        spread = Spread(place, own.at[part], rates.at[year, part], spread_sems.at[part])
        spread.start()
        return spread

    for part in range(PARTS):
        for year in range(2):
            returns(part, year)
        first_rates(part)
        if part == 0:
            advance(0, 0)
            t0 = totals(0)
            t0.start()
        else:
            t0.add_x()
            t0.add_z()
            advance(1, 0)
            t1 = totals(1)
            t1.start()
    for year in range(1, years):
        if year == 1:
            returns(0, 2)
        t1.add_x()
        s0 = declare(t0, year, 0)
        t1.add_z()
        if year == 1:
            returns(1, 2)
        s0.relay_z()
        s0.relay_x()
        s1 = declare(t1, year, 1)
        s0.finish()
        t0.settle()
        if year < years - 1:
            advance(0, year)
            t0 = totals(0)
            t0.start()
        s1.relay_z()
        if year < years - 1:
            t0.add_x()
        s1.relay_x()
        if year < years - 1:
            t0.add_z()
        s1.finish()
        t1.settle()
        if year < years - 1:
            advance(1, year)
            t1 = totals(1)
            t1.start()


def main(rows, tables, loadings, holdings, shocks, draws, size):
    secs, funds = holdings.shape
    years, factors, paths = shocks.shape
    count = rows[0].shape[1]
    depth = size // 4
    width = paths // PARTS
    own_rows = funds // size
    f32, bf16 = jnp.float32, jnp.bfloat16
    part = pltpu.VMEM((PARTS, depth, 2, own_rows, width), f32)
    vmem = pl.BlockSpec(memory_space=pltpu.VMEM)
    smem = pl.BlockSpec(memory_space=pltpu.SMEM)
    anywhere = pl.BlockSpec(memory_space=pl.ANY)
    dma = pltpu.SemaphoreType.DMA
    return pl.pallas_call(
        main_kernel,
        out_shape=(
            jax.ShapeDtypeStruct((PARTS, count, width), f32),
            jax.ShapeDtypeStruct((PARTS, count, width), f32),
            jax.ShapeDtypeStruct((years, PARTS, funds, width), f32),
            jax.ShapeDtypeStruct((years, PARTS, depth, 2, 2, own_rows, width), f32),
            jax.ShapeDtypeStruct((count, 2 * funds), bf16),
            jax.ShapeDtypeStruct((count, funds), f32),
        ),
        in_specs=[smem] * 2 + [vmem] * 8 + [anywhere] * 2,
        out_specs=(vmem,) * 6,
        scratch_shapes=[
            pltpu.VMEM((years, factors, paths), f32),
            pltpu.VMEM((years - 1, count, paths), bf16),
            pltpu.VMEM((2 * secs + 16, funds), f32),
            pltpu.VMEM((depth, 2, 2, 2 * secs + 16, funds), f32),
            pltpu.VMEM((depth, 4 * secs, 2 * factors), bf16),
            pltpu.VMEM((depth, 2 * funds, 4 * secs), bf16),
            pltpu.VMEM((years, funds, count), bf16),
            pltpu.VMEM((funds, funds), f32),
            pltpu.VMEM((PARTS, 2, depth, 2, 2, own_rows, width), f32),
            pltpu.VMEM((PARTS, depth, 2, 2, own_rows, width), f32),
            part,
            part,
            part,
            part,
            pltpu.VMEM((PARTS, own_rows, width), f32),
            dma((2,)),
            dma((2, 4 * depth)),
            dma((PARTS, 2, 4 * depth)),
            dma((PARTS, 2, 4 * depth)),
        ],
        compiler_params=pltpu.CompilerParams(
            collective_id=0, has_side_effects=True, vmem_limit_bytes=60 << 20
        ),
        name="project",
    )(*tables, *rows, loadings, holdings, shocks, draws)


def last_kernel(year, member, columns, assets, liability, fund_ret, rates, draws, held, owed):
    growth_of = stacked(fund_ret[...])
    credit_of = stacked(rates[...])
    for first in range(0, member.shape[0], ROWS):
        rows = slice(first, first + ROWS)
        held[rows], owed[rows] = year_step(
            member[rows],
            None,
            columns[rows, 4 + year : 5 + year],
            columns[rows, 1:2],
            columns[rows, 0:1],
            growth_of,
            credit_of,
            draws[rows],
            assets[rows],
            liability[rows],
        )


def last(member, columns, assets, liability, fund_ret, rates, draws):
    years, parts, funds, width = fund_ret.shape
    count = member.shape[0]
    inner = width // LANES
    state = pl.BlockSpec((None, count, LANES), lambda p, b: (p, 0, b))
    table = pl.BlockSpec((None, None, funds, LANES), lambda p, b: (years - 1, p, 0, b))
    out = pl.BlockSpec((count, LANES), lambda p, b: (0, p * inner + b))
    result = jax.ShapeDtypeStruct((count, parts * width), jnp.float32)
    return pl.pallas_call(
        functools.partial(last_kernel, years - 1),
        grid=(parts, inner),
        out_shape=(result, result),
        in_specs=[
            pl.BlockSpec(member.shape, lambda p, b: (0, 0)),
            pl.BlockSpec(columns.shape, lambda p, b: (0, 0)),
            state,
            state,
            table,
            table,
            pl.BlockSpec((None, count, LANES), lambda p, b: (years - 1, 0, p * inner + b)),
        ],
        out_specs=(out, out),
        name="last",
    )(member, columns, assets, liability, fund_ret, rates, draws)


def local(
    shocks,
    loadings,
    sec_drift,
    holdings,
    fund_of,
    product_type,
    term_years,
    asset_start,
    liab_start,
    base_lapse,
    guarantee,
    lapse_draw,
):
    years, _, paths = shocks.shape
    funds = holdings.shape[1]
    size = lax.axis_size("pol")
    vectors = (fund_of, product_type, term_years, asset_start, liab_start, sec_drift)
    rows = [vector.reshape(1, -1) for vector in vectors]
    draws = jnp.transpose(lapse_draw, (1, 0, 2))
    assets, liability, fund_ret, rates, member, columns = main(
        rows, (base_lapse, guarantee), loadings, holdings, shocks, draws, size
    )
    width = paths // PARTS
    rates = rates.reshape(years, PARTS, funds, width)
    assets, liability = last(member, columns, assets, liability, fund_ret, rates, draws)
    owned = paths // size
    first_path = lax.axis_index("pol") * owned
    mine = lax.dynamic_slice(
        rates, (0, first_path // width, 0, first_path % width), (years, 1, funds, owned)
    )
    return assets, liability, mine.reshape(years, funds, owned)


def solution(mesh):
    in_specs = (
        P("grp", None, None),
        P("pol", None),
        P("pol"),
        P("pol", None),
        P("pol", None),
        P("pol"),
        P("pol"),
        P("pol"),
        P("pol"),
        P(),
        P(),
        P("pol", "grp", None),
    )
    out_specs = (P("pol", "grp"), P("pol", "grp"), P("grp", None, "pol"))
    return jax.shard_map(local, mesh=mesh, in_specs=in_specs, out_specs=out_specs, check_vma=False)
```

```python
import functools

import jax
import jax.numpy as jnp
from jax import lax
from jax.experimental import pallas as pl
from jax.experimental.pallas import tpu as pltpu
from jax.sharding import PartitionSpec as P

MESH = pl.DeviceIdType.MESH
HIGHEST = lax.Precision.HIGHEST
PARTS = 2
LANES = 256
ROWS = 256
EARLY = 2


def crediting(ra, rl):
    x = 20.0 * (ra / rl - 1.05)
    return 0.01 + (jnp.maximum(x, 0.0) + jnp.log1p(jnp.exp(-jnp.abs(x)))) / 20.0


def split(x):
    high = x.astype(jnp.bfloat16)
    return high, (x - high.astype(jnp.float32)).astype(jnp.bfloat16)


def stacked(x):
    return jnp.concatenate(split(x), axis=0)


def dot(a, b):
    return jnp.dot(a, b, preferred_element_type=jnp.float32)


class Place:
    def __init__(self, depth):
        me = lax.axis_index("pol")
        self.depth = depth
        self.core = lax.rem(me, 2)
        self.x = lax.rem(me // 2, 2)
        self.z = me // 4

    def device(self, z, x, core):
        return (z * 2 + x) * 2 + core

    def ahead(self, t):
        return lax.rem(self.z + t, self.depth)

    def behind(self, t):
        return lax.rem(self.z + self.depth - t, self.depth)

    def to_core(self):
        return self.device(self.z, self.x, 1 - self.core)

    def to_x(self):
        return self.device(self.z, 1 - self.x, self.core)

    def to_z(self, t):
        return self.device(self.ahead(t), self.x, self.core)

    def greet(self):
        barrier = pltpu.get_barrier_semaphore()
        others = [self.to_core(), self.to_x()] + [self.to_z(t) for t in range(1, self.depth)]
        for other in others:
            pl.semaphore_signal(barrier, inc=1, device_id={"pol": other}, device_id_type=MESH)
        pl.semaphore_wait(barrier, len(others))


def send(src, dst, sems, at, device):
    copy = pltpu.make_async_remote_copy(
        src_ref=src,
        dst_ref=dst,
        send_sem=sems.at[0, at],
        recv_sem=sems.at[1, at],
        device_id={"pol": device},
        device_id_type=MESH,
    )
    copy.start()
    return copy


class Spread:
    def __init__(self, place, own, every, sems):
        self.p, self.own, self.every, self.sems = place, own, every, sems

    def start(self):
        p, n = self.p, self.p.depth
        slot = self.every.at[p.z, p.x, p.core]
        self.along = [send(self.own, slot, self.sems, t, p.to_z(t)) for t in range(1, n)]
        self.across = {0: send(self.own, slot, self.sems, n, p.to_x())}
        self.pair = {0: send(self.own, slot, self.sems, 2 * n, p.to_core())}
        self.every[p.z, p.x, p.core] = self.own[...]

    def arrive_z(self, t):
        p, n = self.p, self.p.depth
        self.along[t - 1].wait_recv()
        slot = self.every.at[p.behind(t), p.x, p.core]
        self.across[t] = send(slot, slot, self.sems, n + t, p.to_x())
        self.pair[t] = send(slot, slot, self.sems, 2 * n + t, p.to_core())

    def arrive_x(self, t):
        p, n = self.p, self.p.depth
        self.across[t].wait_recv()
        slot = self.every.at[p.behind(t), 1 - p.x, p.core]
        self.pair[n + t] = send(slot, slot, self.sems, 3 * n + t, p.to_core())

    def arrive_pair(self, t):
        self.pair[t].wait_recv()
        self.pair[self.p.depth + t].wait_recv()

    def relay_z(self):
        for t in range(1, self.p.depth):
            self.arrive_z(t)

    def relay_x(self):
        for t in range(self.p.depth):
            self.arrive_x(t)

    def finish(self):
        for t in range(self.p.depth):
            self.arrive_pair(t)
        self.settle()

    def settle(self):
        for copy in self.along + list(self.across.values()) + list(self.pair.values()):
            copy.wait_send()


class Totals:
    def __init__(self, place, sums, pair_in, x_out, x_in, z_out, z_in, sems):
        self.p, self.sums, self.pair_in, self.sems = place, sums, pair_in, sems
        self.x_out, self.x_in, self.z_out, self.z_in = x_out, x_in, z_out, z_in
        self.order = list(range(1, place.depth)) + [0]

    def start(self):
        p, n = self.p, self.p.depth
        self.pair = {}
        for x, base in ((1 - p.x, 0), (p.x, n)):
            for t in self.order:
                z = p.ahead(t)
                self.pair[base + t] = send(
                    self.sums.at[:, z, x, 1 - p.core],
                    self.pair_in.at[z, x],
                    self.sems,
                    base + t,
                    p.to_core(),
                )

    def add_x(self):
        p, n = self.p, self.p.depth
        self.across = {}
        for t in self.order:
            z = p.ahead(t)
            self.pair[t].wait_recv()
            self.x_out[t] = self.sums[:, z, 1 - p.x, p.core] + self.pair_in[z, 1 - p.x]
            self.across[t] = send(
                self.x_out.at[t], self.x_in.at[t], self.sems, 2 * n + t, p.to_x()
            )

    def chip_sum(self, t):
        p, n = self.p, self.p.depth
        z = p.ahead(t)
        self.pair[n + t].wait_recv()
        self.across[t].wait_recv()
        return self.sums[:, z, p.x, p.core] + self.pair_in[z, p.x] + self.x_in[t]

    def add_z(self):
        p, n = self.p, self.p.depth
        self.along = {}
        for t in range(1, n):
            self.z_out[t] = self.chip_sum(t)
            self.along[t] = send(
                self.z_out.at[t], self.z_in.at[t], self.sems, 3 * n + t, p.to_z(t)
            )

    def finish(self):
        total = self.chip_sum(0)
        for t in range(1, self.p.depth):
            self.along[t].wait_recv()
            total = total + self.z_in[t]
        return total

    def settle(self):
        for group in (self.pair, self.across, self.along):
            for copy in group.values():
                copy.wait_send()


def year_step(member, force, base, floor, growth_of, credit_of, draw, assets, liability):
    growth = dot(member, growth_of)
    credit = jnp.maximum(dot(member, credit_of), floor)
    assets = assets * (1.0 + force * growth)
    lapse = force * jnp.minimum(
        base * (0.5 + draw.astype(jnp.float32)) * jnp.exp(5.0 * (growth - credit)), 0.5
    )
    stay = 1.0 - lapse
    return assets * stay, liability * (1.0 + force * credit) * stay


def main_kernel(
    base_lapse,
    guarantee,
    fund_row,
    type_row,
    term_row,
    asset_row,
    liab_row,
    drift_row,
    loadings,
    holdings,
    shocks_hbm,
    draws_hbm,
    assets,
    liability,
    mine,
    fund_ret,
    rates,
    member,
    columns,
    shocks,
    pieces,
    draws,
    packed,
    every,
    extra_own,
    extra_every,
    loads,
    holds,
    hots,
    extra_columns,
    sums,
    pair_in,
    x_out,
    x_in,
    z_out,
    z_in,
    own,
    local_sems,
    gather_sems,
    extra_sems,
    total_sems,
    spread_sems,
):
    depth = every.shape[0]
    secs, funds = holdings.shape
    count = fund_row.shape[1]
    years = shocks.shape[0]
    width = shocks.shape[2] // PARTS
    groups, group_secs, _ = loads.shape
    place = Place(depth)

    fetch_shocks = pltpu.make_async_copy(shocks_hbm, shocks, local_sems.at[0])
    fetch_draws = pltpu.make_async_copy(draws_hbm, draws, local_sems.at[1])
    fetch_shocks.start()
    fetch_draws.start()
    packed[:secs] = loadings[...]
    packed[secs:] = holdings[...]
    place.greet()
    gather = Spread(place, packed, every, gather_sems)
    gather.start()

    fund_id = lax.broadcasted_iota(jnp.int32, (funds, count), 0)
    hot = fund_row[...] == fund_id
    hot_rows = hot.astype(jnp.float32)
    floor = jnp.zeros((1, count), jnp.float32)
    base = jnp.zeros((1, count), jnp.float32)
    for kind in range(guarantee.shape[0]):
        same = type_row[...] == kind
        floor = jnp.where(same, guarantee[kind], floor)
        base = jnp.where(same, base_lapse[kind], base)
    in_force = [(term_row[...] > year).astype(jnp.float32) for year in range(years)]
    row = lax.broadcasted_iota(jnp.int32, (funds, count), 0)
    table = jnp.zeros((funds, count), jnp.float32)
    for at, values in enumerate([floor, base, asset_row[...], liab_row[...]] + in_force):
        table = jnp.where(row == at, values, table)
    columns[...] = table.T
    starts = jnp.concatenate(
        [in_force[0] * asset_row[...], liab_row[...], jnp.zeros((6, count), jnp.float32)], axis=0
    )
    member_f32 = hot_rows.T
    start_sums = jnp.dot(starts, member_f32, precision=HIGHEST)
    drifts = jnp.broadcast_to(drift_row[...], (8, secs))
    drift_sums = jnp.dot(drifts, holdings[...], precision=HIGHEST)
    extra_own[:8] = drift_sums
    extra_own[8:] = start_sums
    extras = Spread(place, extra_own, extra_every, extra_sems)
    extras.start()
    fetch_shocks.wait()
    for year in range(years):
        for part in range(PARTS):
            pieces[year, part] = stacked(shocks[year, :, part * width : (part + 1) * width])

    def term_of(at, year, part):
        exposure = dot(loads[at, :, : 2 * funds], pieces[year, part]) + dot(
            loads[at, :, 2 * funds :], pieces[year, part, :funds]
        )
        t_high, t_low = split(0.25 * jnp.tanh(exposure))
        both = dot(holds[at], t_high)
        return both[:funds] + both[funds:] + dot(holds[at, :funds], t_low)

    def compute(t):
        at = place.behind(t)
        block = every[at]
        high, low = split(block[:, :, :secs].reshape(group_secs, funds))
        loads[at] = jnp.concatenate([high, high, low], axis=1)
        high, low = split(block[:, :, secs:].reshape(group_secs, funds).T)
        holds[at] = jnp.concatenate([high, low], axis=0)

        def step(i, _):
            year = i // PARTS
            part = i - year * PARTS
            term = term_of(at, year, part)
            if t > 0:
                term = term + fund_ret[year, part]
            if t == depth - 1:
                term = term + extra_columns[:, 0:1]
            fund_ret[year, part] = term
            return 0

        lax.fori_loop(0, EARLY * PARTS, step, 0)

    for t in range(depth):
        if t + 1 < depth:
            gather.arrive_z(t + 1)
        gather.arrive_x(t)
        if t == 0:
            narrow = member_f32.astype(jnp.bfloat16)
            member[...] = jnp.concatenate([narrow, narrow], axis=1)
            hots[0] = hot_rows.astype(jnp.bfloat16)
            for year in range(1, years):
                hots[year] = jnp.where(in_force[year] > 0.0, hot_rows, 0.0).astype(jnp.bfloat16)
        gather.arrive_pair(t)
        if t == depth - 1:
            extras.relay_z()
            extras.relay_x()
            extras.finish()
            extra = jnp.zeros((16, funds), jnp.float32)
            for device in range(4 * depth):
                extra += extra_every[device // 4, (device // 2) % 2, device % 2]
            extra_columns[...] = jnp.concatenate(
                [extra, jnp.zeros((funds - 16, funds), jnp.float32)], axis=0
            ).T
        compute(t)
    gather.settle()
    fetch_draws.wait()

    def returns(part, year):
        total = lax.fori_loop(
            0,
            groups,
            lambda at, total: total + term_of(at, year, part),
            jnp.zeros((funds, width), jnp.float32),
        )
        fund_ret[year, part] = total + extra_columns[:, 0:1]

    def first_rates(part):
        declared = crediting(
            extra_columns[:, 8:9] * (1.0 + fund_ret[0, part]), extra_columns[:, 9:10]
        )
        rates[0, part] = declared.reshape(rates.shape[2:])

    def advance(part, year):
        def step(block, _):
            lanes = pl.ds(pl.multiple_of(block * LANES, LANES), LANES)
            whole = pl.ds(pl.multiple_of(part * width + block * LANES, LANES), LANES)
            growth_of = stacked(fund_ret[year, part, :, lanes])
            declared = rates[year, part, :, :, :, :, lanes].reshape(funds, LANES)
            credit_of = stacked(declared)
            asset_sum = jnp.zeros((funds, LANES), jnp.float32)
            liab_sum = jnp.zeros((funds, LANES), jnp.float32)
            for first in range(0, count, ROWS):
                rows = slice(first, first + ROWS)
                if year == 0:
                    held = jnp.broadcast_to(columns[rows, 2:3], (ROWS, LANES))
                    owed = jnp.broadcast_to(columns[rows, 3:4], (ROWS, LANES))
                else:
                    held = assets[rows, whole]
                    owed = liability[rows, whole]
                held, owed = year_step(
                    member[rows],
                    columns[rows, 4 + year : 5 + year],
                    columns[rows, 1:2],
                    columns[rows, 0:1],
                    growth_of,
                    credit_of,
                    draws[year, rows, whole],
                    held,
                    owed,
                )
                assets[rows, whole] = held
                liability[rows, whole] = owed
                if year == years - 1:
                    continue
                high, low = split(held)
                pick = hots[year + 1, :, rows]
                asset_sum += dot(pick, high) + dot(pick, low)
                high, low = split(owed)
                pick = hots[0, :, rows]
                liab_sum += dot(pick, high) + dot(pick, low)
            if year == years - 1:
                return 0
            asset_sum = asset_sum * (1.0 + fund_ret[year + 1, part, :, lanes])
            shape = sums.shape[2:6] + (LANES,)
            sums[part, 0, :, :, :, :, lanes] = asset_sum.reshape(shape)
            sums[part, 1, :, :, :, :, lanes] = liab_sum.reshape(shape)
            return 0

        lax.fori_loop(0, width // LANES, step, 0)

    def totals(part):
        return Totals(
            place,
            sums.at[part],
            pair_in.at[part],
            x_out.at[part],
            x_in.at[part],
            z_out.at[part],
            z_in.at[part],
            total_sems.at[part],
        )

    def declare(total, year, part):
        summed = total.finish()
        own[part] = crediting(summed[0], summed[1])
        spread = Spread(place, own.at[part], rates.at[year, part], spread_sems.at[part])
        spread.start()
        return spread

    first_rates(0)
    advance(0, 0)
    t0 = totals(0)
    t0.start()
    first_rates(1)
    t0.add_x()
    advance(1, 0)
    t0.add_z()
    t1 = totals(1)
    t1.start()
    for year in range(1, years):
        again = year < years - 1
        t1.add_x()
        if year >= EARLY - 1 and again:
            returns(0, year + 1)
        s0 = declare(t0, year, 0)
        t1.add_z()
        if year >= EARLY - 1 and again:
            returns(1, year + 1)
        s0.relay_z()
        s0.relay_x()
        s1 = declare(t1, year, 1)
        s0.finish()
        t0.settle()
        advance(0, year)
        if again:
            t0 = totals(0)
            t0.start()
        s1.relay_z()
        if again:
            t0.add_x()
        s1.relay_x()
        if again:
            t0.add_z()
        s1.finish()
        t1.settle()
        advance(1, year)
        if again:
            t1 = totals(1)
            t1.start()

    owned = mine.shape[2]
    first = lax.axis_index("pol") * owned
    tile = min(width, 128)
    inside = lax.rem(first, width)
    start = pl.multiple_of((inside // tile) * tile, tile)
    turn = lax.rem(inside, tile)
    for year in range(years):
        near = rates[year, first // width, :, :, :, :, pl.ds(start, tile)].reshape(funds, tile)
        chosen = near[:, :owned]
        for at in range(owned, tile, owned):
            chosen = jnp.where(turn == at, near[:, at : at + owned], chosen)
        mine[year] = chosen


def main(rows, tables, loadings, holdings, shocks, draws, size):
    secs, funds = holdings.shape
    years, factors, paths = shocks.shape
    count = rows[0].shape[1]
    depth = size // 4
    width = paths // PARTS
    own_rows = funds // size
    f32, bf16 = jnp.float32, jnp.bfloat16
    part = pltpu.VMEM((PARTS, depth, 2, own_rows, width), f32)
    vmem = pl.BlockSpec(memory_space=pltpu.VMEM)
    smem = pl.BlockSpec(memory_space=pltpu.SMEM)
    anywhere = pl.BlockSpec(memory_space=pl.ANY)
    dma = pltpu.SemaphoreType.DMA
    return pl.pallas_call(
        main_kernel,
        out_shape=(
            jax.ShapeDtypeStruct((count, paths), f32),
            jax.ShapeDtypeStruct((count, paths), f32),
            jax.ShapeDtypeStruct((years, funds, paths // size), f32),
        ),
        in_specs=[smem] * 2 + [vmem] * 8 + [anywhere] * 2,
        out_specs=(vmem,) * 3,
        scratch_shapes=[
            pltpu.VMEM((years, PARTS, funds, width), f32),
            pltpu.VMEM((years, PARTS, depth, 2, 2, own_rows, width), f32),
            pltpu.VMEM((count, 2 * funds), bf16),
            pltpu.VMEM((count, funds), f32),
            pltpu.VMEM((years, factors, paths), f32),
            pltpu.VMEM((years, PARTS, 2 * factors, width), bf16),
            pltpu.VMEM((years, count, paths), bf16),
            pltpu.VMEM((2 * secs, funds), f32),
            pltpu.VMEM((depth, 2, 2, 2 * secs, funds), f32),
            pltpu.VMEM((16, funds), f32),
            pltpu.VMEM((depth, 2, 2, 16, funds), f32),
            pltpu.VMEM((depth, 4 * secs, 3 * factors), bf16),
            pltpu.VMEM((depth, 2 * funds, 4 * secs), bf16),
            pltpu.VMEM((years, funds, count), bf16),
            pltpu.VMEM((funds, funds), f32),
            pltpu.VMEM((PARTS, 2, depth, 2, 2, own_rows, width), f32),
            pltpu.VMEM((PARTS, depth, 2, 2, own_rows, width), f32),
            part,
            part,
            part,
            part,
            pltpu.VMEM((PARTS, own_rows, width), f32),
            dma((2,)),
            dma((2, 4 * depth)),
            dma((2, 4 * depth)),
            dma((PARTS, 2, 4 * depth)),
            dma((PARTS, 2, 4 * depth)),
        ],
        compiler_params=pltpu.CompilerParams(
            collective_id=0, has_side_effects=True, vmem_limit_bytes=60 << 20
        ),
        name="project",
    )(*tables, *rows, loadings, holdings, shocks, draws)


def local(
    shocks,
    loadings,
    sec_drift,
    holdings,
    fund_of,
    product_type,
    term_years,
    asset_start,
    liab_start,
    base_lapse,
    guarantee,
    lapse_draw,
):
    size = lax.axis_size("pol")
    vectors = (fund_of, product_type, term_years, asset_start, liab_start, sec_drift)
    rows = [vector.reshape(1, -1) for vector in vectors]
    draws = jnp.transpose(lapse_draw, (1, 0, 2))
    return main(rows, (base_lapse, guarantee), loadings, holdings, shocks, draws, size)


def solution(mesh):
    in_specs = (
        P("grp", None, None),
        P("pol", None),
        P("pol"),
        P("pol", None),
        P("pol", None),
        P("pol"),
        P("pol"),
        P("pol"),
        P("pol"),
        P(),
        P(),
        P("pol", "grp", None),
    )
    out_specs = (P("pol", "grp"), P("pol", "grp"), P("grp", None, "pol"))
    return jax.shard_map(local, mesh=mesh, in_specs=in_specs, out_specs=out_specs, check_vma=False)
```
